512 devices in a mesh: dp: 64 (over x, z, core), tensor: 8 (over y).
Axes of the slice: x: 4, y: 8, z: 8, core: 2. Of those that a mesh axis runs over, the one named last changes fastest.
Arguments:
- q_new: bfloat16 [8192, 8192], P(('dp', 'tensor')), may hold values from -6 to 6
- k_new: bfloat16 [8192, 1024], P(('dp', 'tensor')), may hold values from -8 to 8
- v_new: bfloat16 [8192, 1024], P(('dp', 'tensor')), may hold values from -6 to 6
- hist_kv: bfloat16 [2048, 128, 2, 1024], P('dp', None, None, 'tensor'), may hold values from -8 to 8
- sources: int32 [64, 64, 1], P('dp'), may hold values from 0 to 63; in each aligned block of 64 rows (0 to 63, 64 to 127, ..., all dimensions but the last counted through in order) at most 2 rows name the same one
- block_ids: int32 [64, 64], P('dp'), may hold values from 0 to 31
- hist_len: int32 [64], P('dp'), may hold values from 1 to 64, 3840 in all
Outputs:
- attended: bfloat16 [8192, 8192], P(('dp', 'tensor'))
The draws below stay inside these ranges and needn't reach their ends.
Inputs may be any that keep to these rules, and one draw needn't show every extreme that they name: `sources`: in each group's list no owner is named in more than 2 slots, and some owner is named in exactly 2 slots. `hist_len`: some group has all 64 slots live.
All inputs are finite; a program needn't handle non-finite values.
Results may differ from the reference program's by a relative error of at most 0.0032.
Values may be sent and summed in bfloat16 or wider, within the bound.
No kernel may reach another device: no remote copies, remote signals or barrier semaphores. Data moves between devices by JAX's collectives and lax.ppermute only.
A program may use at most 64 MiB of HBM per device.

```python
import math
import jax
import jax.numpy as jnp
import numpy as np
from jax import lax

HQ = 64
KVH = 8
HD = 128
NEW = 128
HMAX = 64
BLOCK = 128
POOL = 32
CAP = 2
GROUPS = 64
TOKENS = 8192
HIST_BLOCKS = 2048
N_DP = 64


def draw_q_new(key, part):
    shape = (TOKENS, HQ * HD)
    values = jnp.clip(jax.random.normal(jax.random.fold_in(key, 1), shape, jnp.float32), -6.0, 6.0)
    return values.astype(jnp.bfloat16)


def draw_hist_kv(key, part):
    shape = (HIST_BLOCKS, BLOCK, KVH * HD)
    keys_part = jnp.clip(2.5 * jax.random.normal(jax.random.fold_in(key, 2), shape, jnp.float32), -8.0, 8.0)
    vals_part = jnp.clip(jax.random.normal(jax.random.fold_in(key, 3), shape, jnp.float32), -6.0, 6.0)
    return jnp.stack([keys_part, vals_part], axis=2).astype(jnp.bfloat16)


def plant(entries, rng, least, high):
    longest = entries.shape.index(max(entries.shape))
    spots = []
    for shift in (0, 1):
        where = [jax.random.randint(jax.random.fold_in(rng, axis), (), 0, length) for axis, length in enumerate(entries.shape)]
        where[longest] = (where[longest] + shift) % entries.shape[longest]
        spots.append(tuple(where))
    return entries.at[spots[0]].set(least).at[spots[1]].set(high)


def shard_levels(key, extent, shards, low, top_value):
    factor_of, own = 1.0, jax.random.fold_in(key, 6)
    for dim, shards_of in shards:
        heights = jnp.exp(jax.random.uniform(jax.random.fold_in(own, dim), (shards_of,), jnp.float32, low / len(shards), top_value / len(shards)))
        factor_of = factor_of * jnp.repeat(heights, extent[dim] // shards_of).reshape([-1 if axis == dim else 1 for axis in range(len(extent))])
    return factor_of


def length_profile(count, total, reach, lean):
    portions = [(1 << 20) // math.isqrt(standing ** lean) + 1 for standing in range(2, count + 1)]
    surplus, holding = total - reach - (count - 1), [1] * (count - 1)
    while surplus > 0:
        movable = [i for i in range(count - 1) if holding[i] < reach]
        pool, budget = sum([portions[i] for i in movable]), surplus
        for i in movable:
            addition = min(reach - holding[i], max(1, budget * portions[i] // pool), surplus)
            holding[i] = holding[i] + addition
            surplus = surplus - addition
    return np.array([reach] + holding)


def ragged_sizes(rng, count, total, reach, lean):
    if count == 2:
        one = jax.random.randint(rng, (), max(1, total - reach), min(reach, total - 1) + 1)
        return jnp.stack([one, total - one])
    lengths = jnp.asarray(length_profile(count, total, reach, lean), jnp.int32)
    couples = (count - 1) // 2
    giver, receiver = lengths[1:1 + 2 * couples:2], lengths[2:2 + 2 * couples:2]
    slack = jnp.minimum(giver - 1, reach - receiver)
    passed = jax.random.randint(jax.random.fold_in(rng, 1), (couples,), 0, 1 << 20) % (slack + 1)
    lengths = lengths.at[1:1 + 2 * couples:2].set(giver - passed).at[2:2 + 2 * couples:2].set(receiver + passed)
    return lengths[jax.random.permutation(jax.random.fold_in(rng, 2), count)]


def assign_block(rng, own, number, rows, amount, top, limit, skew):
    order = jax.random.permutation(rng, amount)
    heavy_load, common = load_shares(amount, rows * top, limit, skew, True), load_shares(amount, rows * top, limit, skew, False)
    places = jnp.arange(amount)

    def named(lengths, turn):
        used = int((lengths > 0).sum())
        fixed = max(1, used // 4)
        shifted = fixed + (places - fixed + turn * (used - fixed)) % max(1, amount - fixed)
        return jnp.zeros((amount,), jnp.int32).at[order[jnp.where(places < fixed, places, shifted)]].set(jnp.asarray(lengths, jnp.int32))

    lengths = jnp.where(number % 4 == 0, named(heavy_load, number // 4), named(common, number - number // 4 - 1))
    mixed = jax.random.permutation(jax.random.fold_in(own, 3), amount)
    source_of, receiver = mixed[0:amount // 2 * 2:2], mixed[1:amount // 2 * 2:2]
    margin = jnp.minimum(lengths[source_of] - 1, limit - lengths[receiver]) // 2
    margin = jnp.where((source_of == order[0]) | (receiver == order[0]) | (lengths[receiver] == 0), 0, jnp.maximum(margin, 0))
    shifted = jax.random.randint(jax.random.fold_in(own, 4), (amount // 2,), 0, 1 << 20) % (margin + 1)
    lengths = lengths.at[source_of].add(-shifted).at[receiver].add(shifted)
    members = jnp.searchsorted(jnp.cumsum(lengths), jnp.arange(rows * top), side="right").astype(jnp.int32)
    table = members.reshape(top, rows).T
    table = table[jax.random.permutation(jax.random.fold_in(own, 1), rows)]
    turn = jax.random.randint(jax.random.fold_in(own, 2), (rows, 1), 0, top)
    return jnp.take_along_axis(table, (jnp.arange(top)[None, :] + turn) % top, axis=1)


def load_shares(count, total, limit, slope, full):
    weights = [(1 << 20) // math.isqrt(grade ** slope) + 1 for grade in range(1, count + 1)]
    largest = limit if full else min(limit, max(-(-total // count), total * weights[0] // sum(weights)))
    least = 1 if total - largest >= count - 1 else 0
    given, spare = [largest] + [least] * (count - 1), total - largest - least * (count - 1)
    while spare > 0:
        movable = [i for i in range(1, count) if given[i] < largest] or [i for i in range(1, count) if given[i] < limit]
        mass, left = sum([weights[i] for i in movable]), spare
        for i in movable:
            addition = min(limit - given[i], max(1, left * weights[i] // mass), spare)
            given[i] = given[i] + addition
            spare = spare - addition
    return np.array(given)


def gaussian(rng, extent, width, bound, shards=(), held_as=jnp.bfloat16):
    array = width * jax.random.normal(rng, extent, jnp.float32)
    if shards:
        array = array * shard_levels(rng, extent, shards, -0.22, 0.18)
    return jnp.clip(array, -bound, bound).astype(held_as)


def setup_inputs(seed: int = 0) -> dict:
    key_of = jax.random.split(jax.random.key(seed), 8)
    q_new = draw_q_new(jax.random.fold_in(key_of[7], 71), 0)
    k_new = gaussian(key_of[1], (TOKENS, KVH * HD), 2.5, 8.0, ((0, 512),))
    v_new = gaussian(key_of[2], (TOKENS, KVH * HD), 1.0, 6.0, ((0, 512),))
    hist_kv = draw_hist_kv(jax.random.fold_in(key_of[7], 71), 0)
    sources_keys = jax.random.split(jax.random.fold_in(key_of[4], 1), GROUPS * HMAX // HMAX)
    sources_turns = jax.random.permutation(jax.random.fold_in(key_of[4], 3), GROUPS * HMAX // HMAX)
    sources = jax.vmap(lambda own, number: assign_block(jax.random.fold_in(key_of[4], 2), own, number, HMAX, N_DP, 1, CAP, 2))(sources_keys, sources_turns).reshape((GROUPS, HMAX, 1))
    block_ids = plant(jax.random.randint(key_of[5], (GROUPS, HMAX), 0, POOL), jax.random.fold_in(key_of[5], 1), 0, POOL - 1).astype(jnp.int32)
    hist_len = ragged_sizes(key_of[6], GROUPS, HMAX * N_DP * 15 // 16, HMAX, 2).astype(jnp.int32)
    return {"q_new": q_new, "k_new": k_new, "v_new": v_new, "hist_kv": hist_kv, "sources": sources, "block_ids": block_ids, "hist_len": hist_len}


def reference(q_new, k_new, v_new, hist_kv, sources, block_ids, hist_len):
    group_count = hist_len.shape[0]
    per_kv = HQ // KVH
    score_scale = 1.0 / math.sqrt(HD)

    def one_group(g):
        query_rows = lax.dynamic_slice_in_dim(q_new, g * NEW, NEW, 0).reshape(NEW, KVH, per_kv, HD).astype(jnp.float32)
        fresh_turn_keys = lax.dynamic_slice_in_dim(k_new, g * NEW, NEW, 0).reshape(NEW, KVH, HD).astype(jnp.float32)
        fresh_turn_values = lax.dynamic_slice_in_dim(v_new, g * NEW, NEW, 0).reshape(NEW, KVH, HD).astype(jnp.float32)
        rows = (sources[g, :, 0] * POOL + block_ids[g]).astype(jnp.int32)
        blocks = hist_kv[rows]
        old_keys = blocks[:, :, 0].reshape(HMAX * BLOCK, KVH, HD).astype(jnp.float32)
        prior_turn_values = blocks[:, :, 1].reshape(HMAX * BLOCK, KVH, HD).astype(jnp.float32)
        live = jnp.repeat(jnp.arange(HMAX) < hist_len[g], BLOCK)
        old_scores = jnp.einsum('nhgd,khd->hgnk', query_rows, old_keys) * score_scale
        old_scores = jnp.where(live[None, None, None, :], old_scores, -jnp.inf)
        causal = jnp.arange(NEW)[:, None] >= jnp.arange(NEW)[None, :]
        fresh_turn_scores = jnp.einsum('fusi,pui->usfp', query_rows, fresh_turn_keys) * score_scale
        fresh_turn_scores = jnp.where(causal[None, None], fresh_turn_scores, -jnp.inf)
        top = jnp.maximum(lax.optimization_barrier(jnp.max(old_scores, axis=-1)), lax.optimization_barrier(jnp.max(fresh_turn_scores, axis=-1)))
        old_weights = jnp.exp(old_scores - top[..., None])
        new_weights = jnp.exp(fresh_turn_scores - top[..., None])
        total = lax.optimization_barrier(jnp.sum(old_weights, axis=-1)) + lax.optimization_barrier(jnp.sum(new_weights, axis=-1))
        prior_pass_result = lax.optimization_barrier(old_weights.astype(jnp.bfloat16)).astype(jnp.float32)
        fresh_pass_result = lax.optimization_barrier(new_weights.astype(jnp.bfloat16)).astype(jnp.float32)
        running_sum = jnp.einsum('cmxf,fcu->cmxu', prior_pass_result, prior_turn_values) + jnp.einsum('qaou,uql->qaol', fresh_pass_result, fresh_turn_values)
        result = running_sum / total[..., None]
        result = jnp.transpose(result, (2, 0, 1, 3)).reshape(NEW, HQ * HD)
        return result.astype(jnp.bfloat16)
    outputs = lax.map(one_group, jnp.arange(group_count, dtype=jnp.int32))
    return outputs.reshape(group_count * NEW, HQ * HD)
```

```python
import functools
import math

import jax
import jax.numpy as jnp
from jax import lax
from jax.experimental import pallas as pl
from jax.experimental.pallas import tpu as pltpu
from jax.sharding import PartitionSpec as P

HD = 128
CHUNKS = 4
LOG2E = math.log2(math.e)
NEG = -1e30


def gather_kernel(per_step, first, count, piece, rows_ref, table_ref, out_ref):
    step = pl.program_id(0)
    for g in range(per_step):
        for s in range(count):
            row = rows_ref[step * per_step + g, first + s]
            out_ref[g, pl.ds(piece * s, piece), :] = table_ref[row, pl.ds(0, piece), :]
            out_ref[g, pl.ds(piece * (count + s), piece), :] = table_ref[row, pl.ds(piece, piece), :]


def gather_pieces(rows, table, first, count):
    groups = rows.shape[0]
    piece = table.shape[1] // 2
    per_step = min(8, groups)
    return pl.pallas_call(
        functools.partial(gather_kernel, per_step, first, count, piece),
        out_shape=jax.ShapeDtypeStruct((groups, 2 * piece * count, HD), table.dtype),
        grid_spec=pltpu.PrefetchScalarGridSpec(
            num_scalar_prefetch=1,
            grid=(groups // per_step,),
            in_specs=[pl.BlockSpec(table.shape, lambda i, rows: (0, 0, 0))],
            out_specs=pl.BlockSpec((per_step, 2 * piece * count, HD), lambda i, rows: (i, 0, 0)),
        ),
        compiler_params=pltpu.CompilerParams(vmem_limit_bytes=24 << 20),
        cost_estimate=pl.CostEstimate(
            flops=0, transcendentals=0, bytes_accessed=2 * groups * count * 2 * piece * HD * 2
        ),
        name="gather_pieces",
    )(rows, table)


def fold(q, keys, vals, mask, top, total, acc):
    scale = LOG2E / math.sqrt(HD)
    scores = lax.dot_general(q, keys, (((1,), (1,)), ((), ())), preferred_element_type=jnp.float32)
    scores = jnp.where(mask, scores * scale, NEG)
    new_top = jnp.maximum(top, jnp.max(scores, axis=-1, keepdims=True))
    weights = jnp.exp2(scores - new_top)
    shrink = jnp.exp2(top - new_top)
    total = total * shrink + jnp.sum(weights, axis=-1, keepdims=True)
    acc = acc * shrink + jnp.dot(weights.astype(jnp.bfloat16), vals, preferred_element_type=jnp.float32)
    return new_top, total, acc


def attend_kernel(first, count, piece, start, last, len_ref, *refs):
    refs = list(refs)
    qkv_ref, kv_ref = refs[:2]
    refs = refs[2:]
    if not start:
        stat_in, acc_in = refs[:2]
        refs = refs[2:]
    new = qkv_ref.shape[0]
    heads = (qkv_ref.shape[1] - 2 * HD) // HD
    sources = kv_ref.shape[0]
    half = piece * count
    width = sources * half
    keys = kv_ref[:, :half, :].reshape(width, HD)
    vals = kv_ref[:, half:, :].reshape(width, HD)
    slot = first + lax.rem(lax.broadcasted_iota(jnp.int32, (1, width), 1), half) // piece
    live = slot < len_ref[0]
    for h in range(heads):
        cols = pl.ds(h * HD, HD)
        q = qkv_ref[:, cols]
        if start:
            causal = lax.broadcasted_iota(jnp.int32, (new, new), 0) >= lax.broadcasted_iota(
                jnp.int32, (new, new), 1
            )
            state = (
                jnp.full((new, 1), NEG, jnp.float32),
                jnp.zeros((new, 1), jnp.float32),
                jnp.zeros((new, HD), jnp.float32),
            )
            state = fold(
                q, qkv_ref[:, pl.ds(heads * HD, HD)], qkv_ref[:, pl.ds(heads * HD + HD, HD)], causal, *state
            )
        else:
            state = (stat_in[:, pl.ds(2 * h, 1)], stat_in[:, pl.ds(2 * h + 1, 1)], acc_in[:, cols])
        top, total, acc = fold(q, keys, vals, live, *state)
        if last:
            refs[0][:, cols] = (acc / total).astype(jnp.bfloat16)
        else:
            refs[0][:, pl.ds(2 * h, 1)] = top
            refs[0][:, pl.ds(2 * h + 1, 1)] = total
            refs[1][:, cols] = acc


def attend(hist_len, qkv, kv, state, first, count, piece, last):
    new = qkv.shape[0]
    q_width = qkv.shape[1] - 2 * HD
    width = kv.shape[0] * piece * count
    start = state is None
    inputs = (qkv, kv) if start else (qkv, kv, *state)
    if last:
        out_shape = (jax.ShapeDtypeStruct((new, q_width), jnp.bfloat16),)
    else:
        out_shape = (
            jax.ShapeDtypeStruct((new, HD), jnp.float32),
            jax.ShapeDtypeStruct((new, q_width), jnp.float32),
        )
    return pl.pallas_call(
        functools.partial(attend_kernel, first, count, piece, start, last),
        out_shape=out_shape,
        grid_spec=pltpu.PrefetchScalarGridSpec(
            num_scalar_prefetch=1,
            grid=(1,),
            in_specs=[pl.BlockSpec(x.shape, functools.partial(lambda n, i, l: (0,) * n, x.ndim)) for x in inputs],
            out_specs=[pl.BlockSpec(o.shape, lambda i, l: (0, 0)) for o in out_shape],
        ),
        compiler_params=pltpu.CompilerParams(vmem_limit_bytes=40 << 20),
        cost_estimate=pl.CostEstimate(
            flops=4 * new * q_width * width,
            transcendentals=new * q_width // HD * width,
            bytes_accessed=2 * kv.size + 2 * qkv.size,
        ),
        name="attend",
    )(hist_len, *inputs)


def local(q_new, k_new, v_new, hist_kv, sources, block_ids, hist_len):
    parts = lax.axis_size("tensor")
    groups = lax.axis_size("dp")
    tok, q_width = q_new.shape
    kv_width = k_new.shape[1]
    pool, block_len = hist_kv.shape[:2]
    piece = block_len // groups
    slots = block_ids.shape[1]

    spread = hist_kv.reshape(pool, groups, piece, 2, HD)
    spread = jnp.transpose(spread, (1, 0, 3, 2, 4)).reshape(groups, pool * 2 * piece, HD)
    table = lax.all_to_all(spread, "dp", split_axis=0, concat_axis=0, tiled=True)
    table = table.reshape(groups * pool, 2 * piece, HD)

    rows = lax.all_gather(sources.reshape(1, slots) * pool + block_ids, "dp", axis=0, tiled=True)

    qkv = jnp.concatenate(
        [
            q_new.reshape(tok, parts, q_width // parts),
            k_new.reshape(tok, parts, kv_width // parts),
            v_new.reshape(tok, parts, kv_width // parts),
        ],
        axis=-1,
    )
    qkv = jnp.transpose(qkv, (1, 0, 2))
    qkv = lax.all_to_all(qkv, "tensor", split_axis=0, concat_axis=0, tiled=True)
    qkv = qkv.reshape(parts * tok, -1)

    count = slots // CHUNKS
    arrived = []
    for c in range(CHUNKS):
        picked = gather_pieces(rows, table, c * count, count)
        arrived.append(lax.all_to_all(picked, "dp", split_axis=0, concat_axis=0, tiled=True))
    state = None
    for c in range(CHUNKS):
        state = attend(hist_len, qkv, arrived[c], state, c * count, count, piece, c == CHUNKS - 1)
    result = state[0].reshape(parts, tok, q_width // parts)
    back = lax.all_to_all(result, "tensor", split_axis=0, concat_axis=0, tiled=True)
    return jnp.transpose(back, (1, 0, 2)).reshape(tok, q_width)


def solution(mesh):
    return jax.shard_map(
        local,
        mesh=mesh,
        in_specs=(
            P(("dp", "tensor"), None),
            P(("dp", "tensor"), None),
            P(("dp", "tensor"), None),
            P("dp", None, None, "tensor"),
            P("dp", None, None),
            P("dp", None),
            P("dp"),
        ),
        out_specs=P(("dp", "tensor"), None),
        check_vma=False,
    )
```

```python
import functools
import math

import jax
import jax.numpy as jnp
from jax import lax
from jax.experimental import pallas as pl
from jax.experimental.pallas import tpu as pltpu
from jax.sharding import Mesh
from jax.sharding import PartitionSpec as P

HD = 128
X, Z, C = 4, 8, 2
SCALE = math.log2(math.e) / math.sqrt(HD)
NEG = -1e30
TERMS = 8
TILE = 256
EXTRA = 8


def attend_kernel(start, last, arrays, cap, parts, item_ref, count_ref, home_ref, *refs):
    refs = list(refs)
    stores, refs = refs[:arrays], refs[arrays:]
    q_ref, refs = refs[0], refs[1:]
    if start:
        (key_ref, val_ref), refs = refs[:2], refs[2:]
    else:
        (acc_in, top_in, total_in), refs = refs[:3], refs[3:]
    if last:
        out_ref, buf, scores, top_ref, total_ref, acc_ref, sems = refs
    else:
        acc_out, top_out, total_out, buf, scores, sems = refs
        acc_ref, top_ref, total_ref = acc_out.at[0], top_out.at[0], total_out.at[0]
    group = pl.program_id(0)
    size = stores[0].shape[0]
    rows = parts * HD
    tiles = range(rows // TILE)
    parity = lax.rem(group, 2)
    count = count_ref[group]
    pairs = count // 2
    odd = lax.rem(count, 2)

    def begin(g, par):
        def one(i, _):
            code = item_ref[g, i]
            for a in range(arrays):

                @pl.when(code // size == a)
                def _():
                    pltpu.make_async_copy(stores[a].at[lax.rem(code, size)], buf.at[par, i], sems.at[par, i]).start()

            return 0

        lax.fori_loop(0, count_ref[g], one, 0)

    @pl.when(group == 0)
    def _():
        begin(0, 0)

    @pl.when(group + 1 < pl.num_programs(0))
    def _():
        begin(group + 1, 1 - parity)

    def rows_of(r):
        return pl.ds(r * TILE, TILE)

    def dots(r, keys):
        q = q_ref[0, pl.ds(r * TILE // HD, TILE // HD)].reshape(TILE, HD)
        return lax.dot_general(q, keys, (((1,), (1,)), ((), ())), preferred_element_type=jnp.float32)

    def keys_of(first, many):
        return buf[parity, pl.ds(first, many), 0].reshape(many * HD, HD)

    def vals_of(first, many):
        return buf[parity, pl.ds(first, many), 1].reshape(many * HD, HD)

    if start:
        top_ref[...] = jnp.full(top_ref.shape, NEG, jnp.float32)
        is_home = group == home_ref[0]

        @pl.when(is_home)
        def _():
            keys = key_ref[...].reshape(-1, HD)
            tok = keys.shape[0] // parts
            for r in tiles:
                at = r * TILE + lax.broadcasted_iota(jnp.int32, (TILE, HD), 0)
                token = at // (rows // parts) * tok + lax.rem(at, tok)
                s = jnp.where(lax.broadcasted_iota(jnp.int32, (TILE, HD), 1) <= token, dots(r, keys), NEG)
                scores[cap // 2, rows_of(r), pl.ds(0, HD)] = s
                top_ref[rows_of(r), :] = s

    else:
        top_ref[...] = top_in[0]

    def finish(i, _):
        pltpu.make_async_copy(stores[0].at[0], buf.at[parity, i], sems.at[parity, i]).wait()
        return 0

    lax.fori_loop(0, count, finish, 0)

    def pair_dots(j, _):
        keys = keys_of(2 * j, 2)
        for r in tiles:
            s = dots(r, keys)
            scores[j, rows_of(r), :] = s
            top_ref[rows_of(r), :] = jnp.maximum(top_ref[rows_of(r), :], jnp.maximum(s[:, :HD], s[:, HD:]))
        return 0

    lax.fori_loop(0, pairs, pair_dots, 0)

    @pl.when(odd == 1)
    def _():
        keys = keys_of(count - 1, 1)
        for r in tiles:
            s = dots(r, keys)
            scores[pairs, rows_of(r), pl.ds(0, HD)] = s
            top_ref[rows_of(r), :] = jnp.maximum(top_ref[rows_of(r), :], s)

    for r in tiles:
        top = jnp.max(top_ref[rows_of(r), :], axis=-1, keepdims=True)
        top_ref[rows_of(r), :] = jnp.broadcast_to(top, (TILE, HD))
    if start:
        total_ref[...] = jnp.zeros(total_ref.shape, jnp.float32)
        acc_ref[...] = jnp.zeros(acc_ref.shape, jnp.float32)
    else:
        shrink = jnp.exp2((top_in[0] - top_ref[...]) * SCALE)
        total_ref[...] = total_in[0] * shrink
        acc_ref[...] = acc_in[0] * shrink

    def add(r, w, vals):
        acc_ref[rows_of(r), :] += jnp.dot(w.astype(jnp.bfloat16), vals, preferred_element_type=jnp.float32)

    def single(r, j, vals):
        w = jnp.exp2((scores[j, rows_of(r), pl.ds(0, HD)] - top_ref[rows_of(r), :]) * SCALE)
        total_ref[rows_of(r), :] += w
        add(r, w, vals)

    if start:

        @pl.when(is_home)
        def _():
            for r in tiles:
                single(r, cap // 2, val_ref[...].reshape(-1, HD))

    def pair_sums(j, _):
        vals = vals_of(2 * j, 2)
        for r in tiles:
            top = top_ref[rows_of(r), :]
            w = jnp.exp2((scores[j, rows_of(r), :] - jnp.concatenate([top, top], axis=1)) * SCALE)
            total_ref[rows_of(r), :] += w[:, :HD] + w[:, HD:]
            add(r, w, vals)
        return 0

    lax.fori_loop(0, pairs, pair_sums, 0)

    @pl.when(odd == 1)
    def _():
        for r in tiles:
            single(r, pairs, vals_of(count - 1, 1))

    if not last:
        return
    each = rows // parts
    eye = lax.broadcasted_iota(jnp.int32, (each, HD), 0) == lax.broadcasted_iota(jnp.int32, (each, HD), 1)
    term = lax.broadcasted_iota(jnp.int32, (TERMS, HD), 0)
    for p in range(parts):
        at = pl.ds(p * each, each)
        total = jnp.sum(total_ref[at, :], axis=-1, keepdims=True)
        total = jnp.sum(jnp.where(eye, total, 0.0), axis=0, keepdims=True)
        top = jnp.sum(jnp.where(eye, top_ref[at, :], 0.0), axis=0, keepdims=True)
        some = total > 0
        safe = jnp.where(some, total, 1.0)
        inverse = jnp.where(some, 1.0 / safe, 0.0)
        value = jnp.where(some, top * SCALE + jnp.log2(safe), NEG)
        high = top_bits(value)
        middle = top_bits(value - high)
        low = value - high - middle
        inverse = jnp.transpose(jnp.broadcast_to(inverse, (each, HD)))
        out_ref[p, pl.ds(0, each), :] = (acc_ref[at, :] * inverse).astype(jnp.bfloat16)
        terms = jnp.where(term == 0, high, jnp.where(term == 1, middle, jnp.where(term == 2, low, 0.0)))
        out_ref[p, pl.ds(each, TERMS), :] = terms.astype(jnp.bfloat16)


def top_bits(value):
    shifted = value * 65537.0
    return shifted - (shifted - value)


def attend(items, counts, home, stores, q, kv, state, cap, parts, last):
    groups = q.shape[0]
    rows = parts * HD
    start = state is None

    def block(*s):
        return pl.BlockSpec(s, lambda g, *_: (g,) + (0,) * (len(s) - 1))

    in_specs = [pl.BlockSpec(memory_space=pl.ANY)] * len(stores) + [block(1, parts, HD, HD)]
    inputs = [*stores, q]
    if start:
        heads = kv.shape[2] // (2 * HD)
        tok = HD // parts
        in_specs.append(pl.BlockSpec((parts, tok, HD), lambda g, i, c, h: (0, 0, h[1])))
        in_specs.append(pl.BlockSpec((parts, tok, HD), lambda g, i, c, h: (0, 0, heads + h[1])))
        inputs += [kv, kv]
    else:
        in_specs += [block(1, rows, HD)] * 3
        inputs += list(state)
    scratch = [
        pltpu.VMEM((2, cap, 2, HD, HD), jnp.bfloat16),
        pltpu.VMEM((cap // 2 + int(start), rows, 2 * HD), jnp.float32),
    ]
    if last:
        shape = (groups * parts, rows // parts + TERMS, HD)
        out_shape = [jax.ShapeDtypeStruct(shape, jnp.bfloat16)]
        out_specs = [block(parts, *shape[1:])]
        scratch += [pltpu.VMEM((rows, HD), jnp.float32)] * 3
    else:
        out_shape = [jax.ShapeDtypeStruct((groups, rows, HD), jnp.float32)] * 3
        out_specs = [block(1, rows, HD)] * 3
    work = groups * rows * cap * HD // 2
    return pl.pallas_call(
        functools.partial(attend_kernel, start, last, len(stores), cap, parts),
        out_shape=out_shape,
        grid_spec=pltpu.PrefetchScalarGridSpec(
            num_scalar_prefetch=3,
            grid=(groups,),
            in_specs=in_specs,
            out_specs=out_specs,
            scratch_shapes=scratch + [pltpu.SemaphoreType.DMA((2, cap))],
        ),
        compiler_params=pltpu.CompilerParams(vmem_limit_bytes=60 << 20),
        cost_estimate=pl.CostEstimate(flops=4 * work * HD, transcendentals=work, bytes_accessed=groups * cap * 65536),
        name="attend",
    )(items, counts, home, *inputs)


def combine_kernel(tok, in_ref, out_ref):
    rows = in_ref.shape[2] - TERMS
    spread = jnp.sum(in_ref[:, 0, pl.ds(rows, TERMS), :].astype(jnp.float32), axis=1)
    weights = jnp.exp2(spread - jnp.max(spread, axis=0, keepdims=True))
    weights = jnp.transpose(weights / jnp.sum(weights, axis=0, keepdims=True))
    result = jnp.zeros((rows, HD), jnp.float32)
    for z in range(in_ref.shape[0]):
        result += weights[:, z : z + 1] * in_ref[z, 0, pl.ds(0, rows), :].astype(jnp.float32)
    result = result.astype(jnp.bfloat16)
    for h in range(rows // tok):
        out_ref[:, pl.ds(h * HD, HD)] = result[h * tok : (h + 1) * tok, :]


def combine(partial, tok):
    planes, parts, depth, _ = partial.shape
    width = (depth - TERMS) // tok * HD
    return pl.pallas_call(
        functools.partial(combine_kernel, tok),
        out_shape=jax.ShapeDtypeStruct((tok, parts * width), jnp.bfloat16),
        grid=(parts,),
        in_specs=[pl.BlockSpec((planes, 1, depth, HD), lambda y: (0, y, 0, 0))],
        out_specs=pl.BlockSpec((tok, width), lambda y: (0, y)),
        name="combine",
    )(partial)


def compact(mask, code, cap, filler):
    before = jnp.sum((mask[:, None, :] & jnp.tri(mask.shape[1], k=-1, dtype=bool)[None]).astype(jnp.int32), axis=-1)
    hit = mask[:, None, :] & (before[:, None, :] == jnp.arange(cap)[None, :, None])
    items = jnp.sum(jnp.where(hit, code[:, None, :] - filler, 0), axis=-1) + filler
    return items, jnp.sum(mask.astype(jnp.int32), axis=-1)


def local(q_new, k_new, v_new, hist_kv, sources, block_ids, hist_len):
    parts = lax.axis_size("y")
    planes = lax.axis_size("z")
    x, z, c, y = (lax.axis_index(a) for a in ("x", "z", "c", "y"))
    tok, q_width = q_new.shape
    pool = hist_kv.shape[0]
    half = pool // 2
    slots = block_ids.shape[1]
    up = [(i, (i + 1) % X) for i in range(X)]
    down = [(i, (i - 1) % X) for i in range(X)]
    swap = [(0, 1), (1, 0)]

    own = [jnp.transpose(hist_kv[:half], (0, 2, 1, 3)), jnp.transpose(hist_kv[half:], (0, 2, 1, 3))]
    left = [None, None]
    right = [None, None]
    left[0] = lax.ppermute(own[0], "x", up)
    right[1] = lax.ppermute(own[1], "x", down)
    left[1] = lax.ppermute(own[1], "x", up)
    right[0] = lax.ppermute(own[0], "x", down)
    far = [lax.ppermute(left[0], "x", up), lax.ppermute(right[1], "x", down)]
    q_new, *own = lax.optimization_barrier((q_new, *own))
    own_other, left_other, right_other, far_other = (
        [lax.ppermute(a, "c", swap) for a in pair] for pair in (own, left, right, far)
    )

    heads = q_width // (parts * HD)
    q = jnp.transpose(q_new.reshape(tok, parts, heads, HD), (1, 2, 0, 3)).reshape(parts, heads * tok, HD)
    lists = jnp.concatenate([sources.reshape(1, slots), block_ids, hist_len.reshape(1, 1)], axis=1)
    lists = jnp.pad(lists, ((0, 0), (0, 2 * HD - lists.shape[1]))).reshape(2, HD)
    lists = jnp.pad(lists, ((0, EXTRA - 2), (0, 0))).astype(jnp.bfloat16)
    q = jnp.concatenate([q, jnp.broadcast_to(lists[None], (parts, EXTRA, HD))], axis=1)
    q = jnp.broadcast_to(q[None], (planes, *q.shape)).reshape(planes * parts, *q.shape[1:])
    q = lax.all_to_all(q, ("z", "y"), split_axis=0, concat_axis=0, tiled=True)
    q = q.reshape(planes, parts, *q.shape[1:])

    lists = q[:, 0, HD : HD + 2, :].reshape(planes, 2 * HD).astype(jnp.int32)
    source, block, length = lists[:, :slots], lists[:, slots : 2 * slots], lists[:, 2 * slots : 2 * slots + 1]
    source_x, source_z, other = source // (Z * C), source // C % Z, (source % C != c).astype(jnp.int32)
    step = (source_x - x) % X
    here = (jnp.arange(slots)[None, :] < length) & (source_z == z)
    near_code = (jnp.where(step == 0, 0, jnp.where(step == X - 1, 2, 4)) + other) * pool + block
    near_items, near_counts = compact(here & (step != 2), near_code, 4 * (X - 1), 0)
    far_items, far_counts = compact(here & (step == 2), other * pool + block, 4, 0)

    kv = jnp.pad(jnp.concatenate([k_new, v_new], axis=1), ((0, 3 * tok), (0, 0)))
    kv = lax.all_gather(kv, "y", axis=0, tiled=False)

    home = jnp.stack([z, y])
    near = [*own, *own_other, *left, *left_other, *right, *right_other]
    state = attend(near_items, near_counts, home, near, q, kv, None, 4 * (X - 1), parts, False)
    (partial,) = attend(far_items, far_counts, home, [*far, *far_other], q, None, state, 4, parts, True)
    partial = lax.all_to_all(partial, ("z", "y"), split_axis=0, concat_axis=0, tiled=True)
    return combine(partial.reshape(planes, parts, *partial.shape[1:]), tok)


def solution(mesh):
    mesh = Mesh(mesh.devices.reshape(X, Z, C, -1), ("x", "z", "c", "y"))
    dp = ("x", "z", "c")
    return jax.shard_map(
        local,
        mesh=mesh,
        in_specs=(
            P((*dp, "y"), None),
            P((*dp, "y"), None),
            P((*dp, "y"), None),
            P(dp, None, None, "y"),
            P(dp, None, None),
            P(dp, None),
            P(dp),
        ),
        out_specs=P((*dp, "y"), None),
        check_vma=False,
    )
```

```python
import functools
import math

import jax
import jax.numpy as jnp
from jax import lax
from jax.experimental import pallas as pl
from jax.experimental.pallas import tpu as pltpu
from jax.sharding import Mesh
from jax.sharding import PartitionSpec as P

HD = 128
X, Z, C = 4, 8, 2
SCALE = math.log2(math.e) / math.sqrt(HD)
NEG = -1e30
TERMS = 8
LIMIT = 4000.0
FINE = float(1 << 18)
SHY = 1.0 - 2.0**-13
TILE = 256
EXTRA = 8


def attend_kernel(arrays, cap, parts, item_ref, count_ref, home_ref, *refs):
    stores = refs[:arrays]
    q_ref, key_ref, val_ref, out_ref, buf, scores, top_ref, total_ref, acc_ref, sems = refs[arrays:]
    group = pl.program_id(0)
    rows = acc_ref.shape[0]
    tiles = range(rows // TILE)
    parity = lax.rem(group, 2)
    count = count_ref[group]

    def begin(g, par):
        def one(i, _):
            code = item_ref[g, i]
            store, block = code >> 8, code & 255

            def pick(low, high):
                if high - low == 1:
                    pltpu.make_async_copy(stores[low].at[block], buf.at[par, i], sems.at[par, i]).start()
                    return
                middle = (low + high) // 2
                pl.when(store < middle)(lambda: pick(low, middle))
                pl.when(store >= middle)(lambda: pick(middle, high))

            pick(0, arrays)
            return 0

        lax.fori_loop(0, count_ref[g], one, 0)

    @pl.when(group == 0)
    def _():
        begin(0, 0)

    @pl.when(group + 1 < pl.num_programs(0))
    def _():
        begin(group + 1, 1 - parity)

    def rows_of(r):
        return pl.ds(r * TILE, TILE)

    def dots(r, keys):
        return lax.dot_general(
            q_ref[0, rows_of(r), :], keys, (((1,), (1,)), ((), ())), preferred_element_type=jnp.float32
        )

    def keys_of(first, many):
        return buf[parity, pl.ds(first, many), 0].reshape(many * HD, HD)

    def vals_of(first, many):
        return buf[parity, pl.ds(first, many), 1].reshape(many * HD, HD)

    top_ref[...] = jnp.full(top_ref.shape, NEG, jnp.float32)
    is_home = group == home_ref[0]

    @pl.when(is_home)
    def _():
        keys = key_ref[...].reshape(-1, HD)
        tok = keys.shape[0] // parts
        for r in tiles:
            at = r * TILE + lax.broadcasted_iota(jnp.int32, (TILE, HD), 0)
            token = at // (rows // parts) * tok + lax.rem(at, tok)
            s = jnp.where(lax.broadcasted_iota(jnp.int32, (TILE, HD), 1) <= token, dots(r, keys), NEG)
            scores[cap, rows_of(r), :] = s
            top_ref[rows_of(r), :] = s

    def finish(i, _):
        pltpu.make_async_copy(stores[0].at[0], buf.at[parity, i], sems.at[parity, i]).wait()
        return 0

    lax.fori_loop(0, count, finish, 0)

    def in_steps(step):
        quads = count >> 2
        lax.fori_loop(0, quads, lambda j, _: (step(4 * j, 4), 0)[1], 0)
        pl.when(count & 2 != 0)(lambda: step(4 * quads, 2))
        pl.when(count & 1 != 0)(lambda: step(count - 1, 1))

    def dots_step(first, many):
        keys = keys_of(first, many)
        for r in tiles:
            s = dots(r, keys)
            top = top_ref[rows_of(r), :]
            for i in range(many):
                part = s[:, i * HD : (i + 1) * HD]
                scores[first + i, rows_of(r), :] = part
                top = jnp.maximum(top, part)
            top_ref[rows_of(r), :] = top

    in_steps(dots_step)
    for r in tiles:
        top = jnp.max(top_ref[rows_of(r), :], axis=-1, keepdims=True)
        top_ref[rows_of(r), :] = jnp.broadcast_to(top, (TILE, HD))
    total_ref[...] = jnp.zeros(total_ref.shape, jnp.float32)
    acc_ref[...] = jnp.zeros(acc_ref.shape, jnp.float32)

    def sums(r, first, many, vals):
        top = top_ref[rows_of(r), :]
        w = [jnp.exp2((scores[first + i, rows_of(r), :] - top) * SCALE) for i in range(many)]
        total_ref[rows_of(r), :] += sum(w)
        w = [a.astype(jnp.bfloat16) for a in w]
        w = w[0] if many == 1 else jnp.concatenate(w, axis=1)
        acc_ref[rows_of(r), :] += jnp.dot(w, vals, preferred_element_type=jnp.float32)

    @pl.when(is_home)
    def _():
        for r in tiles:
            sums(r, cap, 1, val_ref[...].reshape(-1, HD))

    def sums_step(first, many):
        vals = vals_of(first, many)
        for r in tiles:
            sums(r, first, many, vals)

    in_steps(sums_step)
    each = rows // parts
    eye = lax.broadcasted_iota(jnp.int32, (each, HD), 0) == lax.broadcasted_iota(jnp.int32, (each, HD), 1)
    term = lax.broadcasted_iota(jnp.int32, (TERMS, HD), 0)
    for p in range(parts):
        at = pl.ds(p * each, each)
        total = jnp.sum(total_ref[at, :], axis=-1, keepdims=True)
        total = jnp.sum(jnp.where(eye, total, 0.0), axis=0, keepdims=True)
        top = jnp.sum(jnp.where(eye, top_ref[at, :], 0.0), axis=0, keepdims=True)
        some = total > 0
        safe = jnp.where(some, total, 1.0)
        inverse = jnp.where(some, 1.0 / safe, 0.0)
        value = jnp.where(some, top * SCALE + jnp.log2(safe), NEG)
        inverse = jnp.transpose(jnp.broadcast_to(inverse, (each, HD)))
        result = acc_ref[at, :] * inverse
        largest = jnp.max(jnp.max(jnp.abs(result), axis=0, keepdims=True), axis=1, keepdims=True)
        power = jnp.clip(jnp.floor(jnp.log2(largest)) + 1.0, -100.0, 15.0)
        fixed = result * (jnp.exp2(15.0 - power) * SHY)
        out_ref[p, pl.ds(0, each), :] = fixed.astype(jnp.int32).astype(jnp.int16)
        value = jnp.floor(jnp.clip(value, -LIMIT, LIMIT) * FINE + 0.5).astype(jnp.int32)
        power = jnp.broadcast_to(power, (1, HD)).astype(jnp.int32)
        terms = jnp.where(term == 0, value >> 16, jnp.where(term == 1, (value & 65535) - 32768, power))
        out_ref[p, pl.ds(each, TERMS), :] = terms.astype(jnp.int16)


def attend(items, counts, home, stores, q, fresh, cap):
    groups = q.shape[0]
    parts, depth, _ = fresh.shape
    rows = parts * HD
    tok = (depth - HD) // 2

    def fresh_block(at):
        return pl.BlockSpec((parts, tok, HD), lambda g, *_: (0, HD // tok + at, 0))

    shape = (groups * parts, rows // parts + TERMS, HD)
    work = groups * rows * cap * HD // 2
    return pl.pallas_call(
        functools.partial(attend_kernel, len(stores), cap, parts),
        out_shape=jax.ShapeDtypeStruct(shape, jnp.int16),
        grid_spec=pltpu.PrefetchScalarGridSpec(
            num_scalar_prefetch=3,
            grid=(groups,),
            in_specs=[
                *[pl.BlockSpec(memory_space=pl.ANY)] * len(stores),
                pl.BlockSpec((1, rows, HD), lambda g, *_: (g, 0, 0)),
                fresh_block(0),
                fresh_block(1),
            ],
            out_specs=pl.BlockSpec((parts, *shape[1:]), lambda g, *_: (g, 0, 0)),
            scratch_shapes=[
                pltpu.VMEM((2, cap, 2, HD, HD), jnp.bfloat16),
                pltpu.VMEM((cap + 1, rows, HD), jnp.float32),
                pltpu.VMEM((rows, HD), jnp.float32),
                pltpu.VMEM((rows, HD), jnp.float32),
                pltpu.VMEM((rows, HD), jnp.float32),
                pltpu.SemaphoreType.DMA((2, cap)),
            ],
        ),
        compiler_params=pltpu.CompilerParams(vmem_limit_bytes=60 << 20),
        cost_estimate=pl.CostEstimate(flops=4 * work * HD, transcendentals=work, bytes_accessed=groups * cap * 65536),
        name="attend",
    )(items, counts, home, *stores, q, fresh, fresh)


def combine_kernel(tok, in_ref, out_ref):
    rows = in_ref.shape[2] - TERMS
    terms = in_ref[:, 0, pl.ds(rows, TERMS), :].astype(jnp.int32)
    spread = (terms[:, 0, :] * 65536 + terms[:, 1, :] + 32768).astype(jnp.float32) * (1.0 / FINE)
    weights = jnp.exp2(spread - jnp.max(spread, axis=0, keepdims=True))
    weights = weights / jnp.sum(weights, axis=0, keepdims=True)
    weights = jnp.transpose(weights * (jnp.exp2(terms[:, 2, :].astype(jnp.float32) - 15.0) / SHY))
    result = jnp.zeros((rows, HD), jnp.float32)
    for z in range(in_ref.shape[0]):
        result += weights[:, z : z + 1] * in_ref[z, 0, pl.ds(0, rows), :].astype(jnp.int32).astype(jnp.float32)
    result = result.astype(jnp.bfloat16)
    for h in range(rows // tok):
        out_ref[:, pl.ds(h * HD, HD)] = result[h * tok : (h + 1) * tok, :]


def combine(partial, tok):
    planes, parts, depth, _ = partial.shape
    width = (depth - TERMS) // tok * HD
    return pl.pallas_call(
        functools.partial(combine_kernel, tok),
        out_shape=jax.ShapeDtypeStruct((tok, parts * width), jnp.bfloat16),
        grid=(parts,),
        in_specs=[pl.BlockSpec((planes, 1, depth, HD), lambda y: (0, y, 0, 0))],
        out_specs=pl.BlockSpec((tok, width), lambda y: (0, y)),
        name="combine",
    )(partial)


def compact(mask, code, cap, filler):
    before = jnp.sum((mask[:, None, :] & jnp.tri(mask.shape[1], k=-1, dtype=bool)[None]).astype(jnp.int32), axis=-1)
    hit = mask[:, None, :] & (before[:, None, :] == jnp.arange(cap)[None, :, None])
    items = jnp.sum(jnp.where(hit, code[:, None, :] - filler, 0), axis=-1) + filler
    return items, jnp.sum(mask.astype(jnp.int32), axis=-1)


def local(q_new, k_new, v_new, hist_kv, sources, block_ids, hist_len):
    parts = lax.axis_size("y")
    planes = lax.axis_size("z")
    x, z, c, y = (lax.axis_index(a) for a in ("x", "z", "c", "y"))
    tok, q_width = q_new.shape
    pool = hist_kv.shape[0]
    half = pool // 2
    slots = block_ids.shape[1]
    up = [(i, (i + 1) % X) for i in range(X)]
    down = [(i, (i - 1) % X) for i in range(X)]
    swap = [(0, 1), (1, 0)]

    own = [jnp.transpose(hist_kv[:half], (0, 2, 1, 3)), jnp.transpose(hist_kv[half:], (0, 2, 1, 3))]
    left = [None, None]
    right = [None, None]
    left[0] = lax.ppermute(own[0], "x", up)
    right[1] = lax.ppermute(own[1], "x", down)
    left[1] = lax.ppermute(own[1], "x", up)
    right[0] = lax.ppermute(own[0], "x", down)
    far = [lax.ppermute(left[0], "x", up), lax.ppermute(right[1], "x", down)]
    heads = q_width // (parts * HD)
    fresh = jnp.concatenate(
        [
            jnp.transpose(a.reshape(tok, parts, -1, HD), (1, 2, 0, 3)).reshape(parts, -1, HD)
            for a in (q_new, k_new, v_new)
        ],
        axis=1,
    )
    fresh = lax.all_to_all(fresh, "y", split_axis=0, concat_axis=0, tiled=True)
    lists = jnp.concatenate([sources.reshape(1, slots), block_ids, hist_len.reshape(1, 1)], axis=1)
    lists = jnp.pad(lists, ((0, 0), (0, EXTRA * HD - lists.shape[1]))).reshape(EXTRA, HD).astype(jnp.bfloat16)
    rows = parts * heads * tok
    q = jnp.concatenate([fresh[:, : heads * tok].reshape(rows, HD), lists], axis=0)
    q, near_left, near_right = lax.optimization_barrier((q, left[0], right[1]))
    q = lax.all_gather(q, "z", axis=0, tiled=False)
    own_other, left_other, right_other, far_other = (
        [lax.ppermute(a, "c", swap) for a in pair] for pair in (own, (near_left, left[1]), (right[0], near_right), far)
    )

    lists = q[:, rows : rows + 2, :].reshape(planes, 2 * HD).astype(jnp.int32)
    source, block, length = lists[:, :slots], lists[:, slots : 2 * slots], lists[:, 2 * slots : 2 * slots + 1]
    source_x, source_z, other = source // (Z * C), source // C % Z, (source % C != c).astype(jnp.int32)
    step = (source_x - x) % X
    here = (jnp.arange(slots)[None, :] < length) & (source_z == z)
    code = (2 * (2 * step + other) + block // half) * 256 + block % half
    items, counts = compact(here, code, 4 * X, 0)
    stores = [*own, *own_other, *right, *right_other, *far, *far_other, *left, *left_other]
    partial = attend(items, counts, z.reshape(1), stores, q, fresh, 4 * X)
    partial = lax.all_to_all(partial, ("z", "y"), split_axis=0, concat_axis=0, tiled=True)
    return combine(partial.reshape(planes, parts, *partial.shape[1:]), tok)


def solution(mesh):
    mesh = Mesh(mesh.devices.reshape(X, Z, C, -1), ("x", "z", "c", "y"))
    dp = ("x", "z", "c")
    return jax.shard_map(
        local,
        mesh=mesh,
        in_specs=(
            P((*dp, "y"), None),
            P((*dp, "y"), None),
            P((*dp, "y"), None),
            P(dp, None, None, "y"),
            P(dp, None, None),
            P(dp, None),
            P(dp),
        ),
        out_specs=P((*dp, "y"), None),
        check_vma=False,
    )
```

```python
import functools
import math

import jax
import jax.numpy as jnp
from jax import lax
from jax.experimental import pallas as pl
from jax.experimental.pallas import tpu as pltpu
from jax.sharding import Mesh
from jax.sharding import PartitionSpec as P

HD = 128
X, Z, C = 4, 8, 2
SCALE = math.log2(math.e) / math.sqrt(HD)
NEG = -1e30
TERMS = 8
LIMIT = 4000.0
FINE = float(1 << 18)
SHY = 1.0 - 2.0**-13
TILE = 256
EXTRA = 8


def attend_kernel(arrays, cap, parts, item_ref, count_ref, home_ref, *refs):
    stores = refs[:arrays]
    q_ref, key_ref, val_ref, out_ref, buf, scores, top_ref, total_ref, acc_ref, sems = refs[arrays:]
    group = pl.program_id(0)
    rows = acc_ref.shape[0]
    tiles = range(rows // TILE)
    parity = lax.rem(group, 2)
    count = count_ref[group]

    def begin(g, par):
        def one(i, _):
            code = item_ref[g, i]
            store, block = code >> 8, code & 255

            def pick(low, high):
                if high - low == 1:
                    pltpu.make_async_copy(stores[low].at[block], buf.at[par, i], sems.at[par, i]).start()
                    return
                middle = (low + high) // 2
                pl.when(store < middle)(lambda: pick(low, middle))
                pl.when(store >= middle)(lambda: pick(middle, high))

            pick(0, arrays)
            return 0

        lax.fori_loop(0, count_ref[g], one, 0)

    @pl.when(group == 0)
    def _():
        begin(0, 0)

    @pl.when(group + 1 < pl.num_programs(0))
    def _():
        begin(group + 1, 1 - parity)

    def rows_of(r):
        return pl.ds(r * TILE, TILE)

    def dots(r, keys):
        return lax.dot_general(
            q_ref[0, rows_of(r), :], keys, (((1,), (1,)), ((), ())), preferred_element_type=jnp.float32
        )

    def keys_of(first, many):
        return buf[parity, pl.ds(first, many), 0].reshape(many * HD, HD)

    def vals_of(first, many):
        return buf[parity, pl.ds(first, many), 1].reshape(many * HD, HD)

    top_ref[...] = jnp.full(top_ref.shape, NEG, jnp.float32)
    is_home = group == home_ref[0]

    @pl.when(is_home)
    def _():
        keys = key_ref[...].reshape(-1, HD)
        tok = keys.shape[0] // parts
        for r in tiles:
            at = r * TILE + lax.broadcasted_iota(jnp.int32, (TILE, HD), 0)
            token = at // (rows // parts) * tok + lax.rem(at, tok)
            s = jnp.where(lax.broadcasted_iota(jnp.int32, (TILE, HD), 1) <= token, dots(r, keys), NEG)
            scores[cap, rows_of(r), :] = s
            top_ref[rows_of(r), :] = s

    def finish(i, _):
        pltpu.make_async_copy(stores[0].at[0], buf.at[parity, i], sems.at[parity, i]).wait()
        return 0

    lax.fori_loop(0, count, finish, 0)

    def in_steps(step):
        quads = count >> 2
        lax.fori_loop(0, quads, lambda j, _: (step(4 * j, 4), 0)[1], 0)
        pl.when(count & 2 != 0)(lambda: step(4 * quads, 2))
        pl.when(count & 1 != 0)(lambda: step(count - 1, 1))

    def dots_step(first, many):
        keys = keys_of(first, many)
        for r in tiles:
            s = dots(r, keys)
            top = top_ref[rows_of(r), :]
            for i in range(many):
                part = s[:, i * HD : (i + 1) * HD]
                scores[first + i, rows_of(r), :] = part
                top = jnp.maximum(top, part)
            top_ref[rows_of(r), :] = top

    in_steps(dots_step)
    for r in tiles:
        top = jnp.max(top_ref[rows_of(r), :], axis=-1, keepdims=True)
        top_ref[rows_of(r), :] = jnp.broadcast_to(top, (TILE, HD))
    total_ref[...] = jnp.zeros(total_ref.shape, jnp.float32)
    acc_ref[...] = jnp.zeros(acc_ref.shape, jnp.float32)

    def sums(r, first, many, vals):
        top = top_ref[rows_of(r), :]
        w = [jnp.exp2((scores[first + i, rows_of(r), :] - top) * SCALE) for i in range(many)]
        total_ref[rows_of(r), :] += sum(w)
        w = [a.astype(jnp.bfloat16) for a in w]
        w = w[0] if many == 1 else jnp.concatenate(w, axis=1)
        acc_ref[rows_of(r), :] += jnp.dot(w, vals, preferred_element_type=jnp.float32)

    @pl.when(is_home)
    def _():
        for r in tiles:
            sums(r, cap, 1, val_ref[...].reshape(-1, HD))

    def sums_step(first, many):
        vals = vals_of(first, many)
        for r in tiles:
            sums(r, first, many, vals)

    in_steps(sums_step)
    each = rows // parts
    eye = lax.broadcasted_iota(jnp.int32, (each, HD), 0) == lax.broadcasted_iota(jnp.int32, (each, HD), 1)
    term = lax.broadcasted_iota(jnp.int32, (TERMS, HD), 0)
    for p in range(parts):
        at = pl.ds(p * each, each)
        total = jnp.sum(total_ref[at, :], axis=-1, keepdims=True)
        total = jnp.sum(jnp.where(eye, total, 0.0), axis=0, keepdims=True)
        top = jnp.sum(jnp.where(eye, top_ref[at, :], 0.0), axis=0, keepdims=True)
        some = total > 0
        safe = jnp.where(some, total, 1.0)
        inverse = jnp.where(some, 1.0 / safe, 0.0)
        value = jnp.where(some, top * SCALE + jnp.log2(safe), NEG)
        inverse = jnp.transpose(jnp.broadcast_to(inverse, (each, HD)))
        result = acc_ref[at, :] * inverse
        largest = jnp.max(jnp.max(jnp.abs(result), axis=0, keepdims=True), axis=1, keepdims=True)
        power = jnp.clip(jnp.floor(jnp.log2(largest)) + 1.0, -100.0, 15.0)
        fixed = result * (jnp.exp2(15.0 - power) * SHY)
        out_ref[p, pl.ds(0, each), :] = fixed.astype(jnp.int32).astype(jnp.int16)
        value = jnp.floor(jnp.clip(value, -LIMIT, LIMIT) * FINE + 0.5).astype(jnp.int32)
        power = jnp.broadcast_to(power, (1, HD)).astype(jnp.int32)
        terms = jnp.where(term == 0, value >> 16, jnp.where(term == 1, (value & 65535) - 32768, power))
        out_ref[p, pl.ds(each, TERMS), :] = terms.astype(jnp.int16)


def attend(items, counts, home, stores, q, fresh, cap):
    groups = q.shape[0]
    parts, depth, _ = fresh.shape
    rows = parts * HD
    tok = (depth - HD) // 2

    def fresh_block(at):
        return pl.BlockSpec((parts, tok, HD), lambda g, *_: (0, HD // tok + at, 0))

    shape = (groups * parts, rows // parts + TERMS, HD)
    work = groups * rows * cap * HD // 2
    return pl.pallas_call(
        functools.partial(attend_kernel, len(stores), cap, parts),
        out_shape=jax.ShapeDtypeStruct(shape, jnp.int16),
        grid_spec=pltpu.PrefetchScalarGridSpec(
            num_scalar_prefetch=3,
            grid=(groups,),
            in_specs=[
                *[pl.BlockSpec(memory_space=pl.ANY)] * len(stores),
                pl.BlockSpec((1, rows, HD), lambda g, *_: (g, 0, 0)),
                fresh_block(0),
                fresh_block(1),
            ],
            out_specs=pl.BlockSpec((parts, *shape[1:]), lambda g, *_: (g, 0, 0)),
            scratch_shapes=[
                pltpu.VMEM((2, cap, 2, HD, HD), jnp.bfloat16),
                pltpu.VMEM((cap + 1, rows, HD), jnp.float32),
                pltpu.VMEM((rows, HD), jnp.float32),
                pltpu.VMEM((rows, HD), jnp.float32),
                pltpu.VMEM((rows, HD), jnp.float32),
                pltpu.SemaphoreType.DMA((2, cap)),
            ],
        ),
        compiler_params=pltpu.CompilerParams(vmem_limit_bytes=60 << 20),
        cost_estimate=pl.CostEstimate(flops=4 * work * HD, transcendentals=work, bytes_accessed=groups * cap * 65536),
        name="attend",
    )(items, counts, home, *stores, q, fresh, fresh)


def combine_kernel(tok, in_ref, out_ref):
    rows = in_ref.shape[2] - TERMS
    heads = rows // tok
    for y in range(in_ref.shape[1]):
        terms = in_ref[:, y, pl.ds(rows, TERMS), :].astype(jnp.int32)
        spread = (terms[:, 0, :] * 65536 + terms[:, 1, :] + 32768).astype(jnp.float32) * (1.0 / FINE)
        weights = jnp.exp2(spread - jnp.max(spread, axis=0, keepdims=True))
        weights = weights / jnp.sum(weights, axis=0, keepdims=True)
        weights = jnp.transpose(weights * (jnp.exp2(terms[:, 2, :].astype(jnp.float32) - 15.0) / SHY))
        result = jnp.zeros((rows, HD), jnp.float32)
        for z in range(in_ref.shape[0]):
            result += weights[:, z : z + 1] * in_ref[z, y, pl.ds(0, rows), :].astype(jnp.int32).astype(jnp.float32)
        result = result.astype(jnp.bfloat16)
        for h in range(heads):
            out_ref[:, pl.ds((y * heads + h) * HD, HD)] = result[h * tok : (h + 1) * tok, :]


def combine(partial, tok, together=4):
    planes, parts, depth, _ = partial.shape
    width = (depth - TERMS) // tok * HD
    return pl.pallas_call(
        functools.partial(combine_kernel, tok),
        out_shape=jax.ShapeDtypeStruct((tok, parts * width), jnp.bfloat16),
        grid=(parts // together,),
        in_specs=[pl.BlockSpec((planes, together, depth, HD), lambda y: (0, y, 0, 0))],
        out_specs=pl.BlockSpec((tok, together * width), lambda y: (0, y)),
        name="combine",
    )(partial)


def compact(mask, code, cap, filler):
    before = jnp.sum((mask[:, None, :] & jnp.tri(mask.shape[1], k=-1, dtype=bool)[None]).astype(jnp.int32), axis=-1)
    hit = mask[:, None, :] & (before[:, None, :] == jnp.arange(cap)[None, :, None])
    items = jnp.sum(jnp.where(hit, code[:, None, :] - filler, 0), axis=-1) + filler
    return items, jnp.sum(mask.astype(jnp.int32), axis=-1)


def local(q_new, k_new, v_new, hist_kv, sources, block_ids, hist_len):
    parts = lax.axis_size("y")
    planes = lax.axis_size("z")
    x, z, c, y = (lax.axis_index(a) for a in ("x", "z", "c", "y"))
    tok, q_width = q_new.shape
    pool = hist_kv.shape[0]
    half = pool // 2
    slots = block_ids.shape[1]
    up = [(i, (i + 1) % X) for i in range(X)]
    down = [(i, (i - 1) % X) for i in range(X)]
    swap = [(0, 1), (1, 0)]

    own = [jnp.transpose(hist_kv[:half], (0, 2, 1, 3)), jnp.transpose(hist_kv[half:], (0, 2, 1, 3))]
    left = [None, None]
    right = [None, None]
    left[0] = lax.ppermute(own[0], "x", up)
    right[1] = lax.ppermute(own[1], "x", down)
    left[1] = lax.ppermute(own[1], "x", up)
    right[0] = lax.ppermute(own[0], "x", down)
    far = [lax.ppermute(left[0], "x", up), lax.ppermute(right[1], "x", down)]
    heads = q_width // (parts * HD)
    fresh = jnp.concatenate(
        [
            jnp.transpose(a.reshape(tok, parts, -1, HD), (1, 2, 0, 3)).reshape(parts, -1, HD)
            for a in (q_new, k_new, v_new)
        ],
        axis=1,
    )
    fresh = lax.all_to_all(fresh, "y", split_axis=0, concat_axis=0, tiled=True)
    lists = jnp.concatenate([sources.reshape(1, slots), block_ids, hist_len.reshape(1, 1)], axis=1)
    lists = jnp.pad(lists, ((0, 0), (0, EXTRA * HD - lists.shape[1]))).reshape(EXTRA, HD).astype(jnp.bfloat16)
    rows = parts * heads * tok
    q = jnp.concatenate([fresh[:, : heads * tok].reshape(rows, HD), lists], axis=0)
    q, near_left, near_right = lax.optimization_barrier((q, left[0], right[1]))
    q = jnp.broadcast_to(q[None], (planes, *q.shape))
    q = lax.all_to_all(q, "z", split_axis=0, concat_axis=0, tiled=True)
    own_other, left_other, right_other, far_other = (
        [lax.ppermute(a, "c", swap) for a in pair] for pair in (own, (near_left, left[1]), (right[0], near_right), far)
    )

    lists = q[:, rows : rows + 2, :].reshape(planes, 2 * HD).astype(jnp.int32)
    source, block, length = lists[:, :slots], lists[:, slots : 2 * slots], lists[:, 2 * slots : 2 * slots + 1]
    source_x, source_z, other = source // (Z * C), source // C % Z, (source % C != c).astype(jnp.int32)
    step = (source_x - x) % X
    here = (jnp.arange(slots)[None, :] < length) & (source_z == z)
    code = (2 * (2 * step + other) + block // half) * 256 + block % half
    items, counts = compact(here, code, 4 * X, 0)
    stores = [*own, *own_other, *right, *right_other, *far, *far_other, *left, *left_other]
    partial = attend(items, counts, z.reshape(1), stores, q, fresh, 4 * X)
    partial = lax.all_to_all(partial, ("z", "y"), split_axis=0, concat_axis=0, tiled=True)
    return combine(partial.reshape(planes, parts, *partial.shape[1:]), tok)


def solution(mesh):
    mesh = Mesh(mesh.devices.reshape(X, Z, C, -1), ("x", "z", "c", "y"))
    dp = ("x", "z", "c")
    return jax.shard_map(
        local,
        mesh=mesh,
        in_specs=(
            P((*dp, "y"), None),
            P((*dp, "y"), None),
            P((*dp, "y"), None),
            P(dp, None, None, "y"),
            P(dp, None, None),
            P(dp, None),
            P(dp),
        ),
        out_specs=P((*dp, "y"), None),
        check_vma=False,
    )
```
